128 devices in a mesh: row: 16 (over x, z_lo, core), col: 8 (over z_hi, y).
Axes of the slice: x: 4, y: 4, z: 4 (z_hi: 2, z_lo: 2; z = z_hi * 2 + z_lo), core: 2. Of those that a mesh axis runs over, the one named last changes fastest.
Arguments:
- out_grad: bfloat16 [512, 16384], P('col', 'row'), may hold values from -6 to 6
- gate_saved: bfloat16 [512, 26624], P('row', 'col'), may hold values from -8 to 8
- up_saved: bfloat16 [512, 26624], P('row', 'col'), may hold values from -6 to 6
- gate_weight: bfloat16 [16384, 26624], P('row', 'col'), may hold values from -0.046875 to 0.046875
- up_weight: bfloat16 [16384, 26624], P('row', 'col'), may hold values from -0.046875 to 0.046875
- down_weight: bfloat16 [26624, 16384], P('col', 'row'), may hold values from -0.0390625 to 0.0390625
Outputs:
- input_grad: bfloat16 [512, 16384], P('col', 'row')
The draws below stay inside these ranges and needn't reach their ends.
All inputs are finite; a program needn't handle non-finite values.
Results may differ from the reference program's by a relative error of at most 0.0049.
Values may be sent and summed in bfloat16 or wider, within the bound.
A program may use at most 128 MiB of HBM per device.

```python
import jax
import jax.numpy as jnp

D = 16384
FF = 26624
TOKENS = 512


def level_of(own_key, extent, shards, smallest, largest):
    def one(position, blocks):
        draws = jax.random.uniform(jax.random.fold_in(jax.random.fold_in(own_key, 6), position), (blocks,), jnp.float32, smallest / len(shards), largest / len(shards))
        return jnp.repeat(jnp.exp(draws), extent[position] // blocks).reshape((-1,) + (1,) * (len(extent) - position - 1))

    level = one(*shards[0])
    for cut in shards[1:]:
        level = level * one(*cut)
    return level


def bell_draw(rng, extent, spread, most, split=(), dtype=jnp.bfloat16):
    entries = spread * jax.random.normal(rng, extent, jnp.float32)
    if split:
        entries = entries * level_of(rng, extent, split, -0.22, 0.18)
    return jnp.clip(entries, -most, most).astype(dtype)


def setup_inputs(seed: int = 0) -> dict:
    streams_of = jax.random.split(jax.random.key(seed), 7)
    return {
        "out_grad": bell_draw(streams_of[0], (TOKENS, D), 1.0, 6.0, ((0, 8), (1, 16))),
        "gate_saved": bell_draw(streams_of[1], (TOKENS, FF), 2.0, 8.0, ((0, 16), (1, 8))),
        "up_saved": bell_draw(streams_of[2], (TOKENS, FF), 1.0, 6.0, ((0, 16), (1, 8))),
        "gate_weight": bell_draw(streams_of[3], (D, FF), D ** -0.5, 0.046875, ((0, 16), (1, 8))),
        "up_weight": bell_draw(streams_of[4], (D, FF), D ** -0.5, 0.046875, ((0, 16), (1, 8))),
        "down_weight": bell_draw(streams_of[5], (FF, D), FF ** -0.5, 0.0390625, ((0, 8), (1, 16))),
    }


def reference(out_grad, gate_saved, up_saved, gate_weight, up_weight, down_weight):
    hidden_grad = jnp.dot(out_grad, down_weight.T, preferred_element_type=jnp.float32)
    gate_float = gate_saved.astype(jnp.float32)
    up_float = up_saved.astype(jnp.float32)
    sigmoid_gate = jax.nn.sigmoid(gate_float)
    up_grad = (hidden_grad * gate_float * sigmoid_gate).astype(jnp.bfloat16)
    gate_grad = (hidden_grad * up_float * sigmoid_gate * (1.0 + gate_float * (1.0 - sigmoid_gate))).astype(jnp.bfloat16)
    total = jnp.dot(gate_grad, gate_weight.T, preferred_element_type=jnp.float32)
    total = total + jnp.dot(up_grad, up_weight.T, preferred_element_type=jnp.float32)
    return total.astype(jnp.bfloat16)
```

```python
import jax
import jax.numpy as jnp
from jax import lax
from jax.experimental import pallas as pl
from jax.experimental.pallas import tpu as pltpu
from jax.sharding import PartitionSpec as P

MESH = pl.DeviceIdType.MESH
F32, BF16 = jnp.float32, jnp.bfloat16

CHUNKS = 2
LANES = 256


def contract_last(left, right):
    return lax.dot_general(
        left, right, (((1,), (1,)), ((), ())), preferred_element_type=F32
    )


class Copies:
    def __init__(self, send_sems, recv_sems):
        self.send_sems, self.recv_sems, self.made = send_sems, recv_sems, {}

    def send(self, name, src, dst, device):
        index = len(self.made)
        copy = pltpu.make_async_remote_copy(
            src_ref=src,
            dst_ref=dst,
            send_sem=self.send_sems.at[index],
            recv_sem=self.recv_sems.at[index],
            device_id=device,
            device_id_type=MESH,
        )
        copy.start()
        self.made[name] = copy

    def arrived(self, *names):
        for name in names:
            self.made[name].wait_recv()

    def finish(self):
        for copy in self.made.values():
            copy.wait_send()


def kernel(
    og, gs, us, gw, uw, dw, out,
    tokens, wd, wg, wu, gv, uv,
    own1, own2, give1, give2, got1, got2,
    xs1, xr1, xs2, xr2, zs1, zr1, keep1, zs2, zr2,
    grads1, grads2, total, ys, yr, keep3, hs, hr,
    local_sems, send_sems, recv_sems,
):
    rows = gs.shape[0] // CHUNKS
    wide1, wide2 = own1.shape[-1], own2.shape[-1]
    half1, half2, half3 = wide1 // 2, wide2 // 2, out.shape[-1] // 2
    row, col = lax.axis_index("row"), lax.axis_index("col")
    x, zl, c = row // 4, (row // 2) % 2, row % 2
    zh, y = col // 4, col % 4

    def at_row(x_, zl_, c_):
        return {"row": (x_ % 4) * 4 + zl_ * 2 + c_}

    def at_col(zh_, y_):
        return {"col": zh_ * 4 + y_ % 4}

    core, zn = at_row(x, zl, 1 - c), at_row(x, 1 - zl, c)
    xp, xm = at_row(x + 1, zl, c), at_row(x + 3, zl, c)
    zp, yp, ym = at_col(1 - zh, y), at_col(zh, y + 1), at_col(zh, y + 3)

    def place(zh_, y_):
        y_ = y_ % 4
        return ((zh_ * 2 + y_ // 2 - x + 4) % 4) * 2 + (y_ % 2 + zl) % 2

    loads = {}

    def load(name, src, dst):
        copy = pltpu.make_async_copy(src, dst, local_sems.at[len(loads)])
        copy.start()
        loads[name] = copy

    mine = place(zh, y)
    for t in range(CHUNKS):
        for c_ in range(2):
            load(
                f"t{t}{c_}",
                og.at[pl.ds(c_ * 32 + t * rows, rows)],
                tokens.at[t, (c_ + c) % 2, mine],
            )
    load("d2", dw.at[pl.ds(wide1, wide2)], wd.at[pl.ds(wide1, wide2)])
    load("d1", dw.at[pl.ds(0, wide1)], wd.at[pl.ds(0, wide1)])
    load("gv", gs, gv)
    load("uv", us, uv)
    load("wg", gw, wg)
    load("wu", uw, wu)

    barrier = pltpu.get_barrier_semaphore()
    peers = (core, zn, xp, xm, zp, yp, ym)
    for peer in peers:
        pl.semaphore_signal(barrier, inc=1, device_id=peer, device_id_type=MESH)
    pl.semaphore_wait(barrier, len(peers))

    net = Copies(send_sems, recv_sems)

    def spread(t, z_, name):
        here = tokens.at[t, :, place(z_, y)]
        net.send(f"a{name}+{t}", here, here, yp)
        net.send(f"a{name}-{t}", here, here, ym)

    def pass_on(t, z_, name):
        net.arrived(f"a{name}+{t}", f"a{name}-{t}")
        left, right = tokens.at[t, 0, place(z_, y + 3)], tokens.at[t, 1, place(z_, y + 1)]
        net.send(f"f{name}+{t}", left, left, yp)
        net.send(f"f{name}-{t}", right, right, ym)

    def gather_1(t):
        loads[f"t{t}0"].wait()
        loads[f"t{t}1"].wait()
        here = tokens.at[t, :, mine]
        net.send(f"az{t}", here, here, zp)
        spread(t, zh, "o")

    def gather_2(t):
        net.arrived(f"az{t}")
        spread(t, 1 - zh, "p")

    def gather_3(t):
        pass_on(t, zh, "o")

    def gather_4(t):
        pass_on(t, 1 - zh, "p")

    def gather_5(t):
        net.arrived(f"fo+{t}", f"fo-{t}", f"fp+{t}", f"fp-{t}")

    def first_dot(t, own, give, got, offset, name):
        wide = own.shape[-1]

        def tile(n, carry):
            left = tokens[t].reshape(16 * rows, -1)
            here = pl.ds(pl.multiple_of(offset + n * LANES, LANES), LANES)
            there = pl.ds(pl.multiple_of(n * LANES, LANES), LANES)
            share = contract_last(left, wd[here, :]).reshape(2, 8, rows, LANES)
            own[t, :, :, there] = share[0]
            give[t, :, :, there] = share[1].astype(BF16)
            return carry

        lax.fori_loop(0, wide // LANES, tile, 0)
        net.send(f"{name}c{t}", give.at[t], got.at[t], core)

    def dot_1(t):
        first_dot(t, own1, give1, got1, 0, "b1")

    def dot_2(t):
        first_dot(t, own2, give2, got2, wide1, "b2")

    def x_out(name, t, xs, xr, part, half):
        for way, m, k, lo, to in (
            (0, 0, 2, 0, xp), (1, 0, 2, half, xm), (0, 1, 1, half, xp), (1, 1, 3, 0, xm),
        ):
            xs[t, way, m] = part(k, lo).astype(BF16)
            net.send(f"{name}{way}{m}{t}", xs.at[t, way, m], xr.at[t, way, m], to)

    def x_on(name, t, xs, xr, part, half):
        for way, k, lo, to in ((0, 1, 0, xp), (1, 3, half, xm)):
            net.arrived(f"{name}{way}0{t}")
            xs[t, way, 2] = (part(k, lo) + xr[t, way, 0].astype(F32)).astype(BF16)
            net.send(f"{name}{way}2{t}", xs.at[t, way, 2], xr.at[t, way, 2], to)

    def x_in(name, t, xr, part, half, finish):
        net.arrived(*(f"{name}{way}{m}{t}" for way in (0, 1) for m in (1, 2)))
        for lo, m in ((0, 2), (half, 1)):
            finish(
                lo,
                part(0, lo)
                + xr[t, 0, m].astype(F32)
                + xr[t, 1, 3 - m].astype(F32),
            )

    def part1(t):
        def part(k, lo):
            here = (t, pl.ds(2 * k, 2), slice(None), pl.ds(lo, half1))
            return own1[here] + got1[here].astype(F32)

        return part

    def part2(t):
        def part(k, lo):
            here = (t, 2 * k, slice(None), pl.ds(lo, half2))
            arrived = zr2[t, k, :, pl.ds(lo, half2)]
            return own2[here] + got2[here].astype(F32) + arrived.astype(F32)

        return part

    def sum1_1(t):
        net.arrived(f"b1c{t}")
        x_out("b1x", t, xs1, xr1, part1(t), half1)

    def sum1_2(t):
        x_on("b1x", t, xs1, xr1, part1(t), half1)

    def sum1_3(t):
        def finish(lo, value):
            zs1[t, :, pl.ds(lo, half1)] = value[1].astype(BF16)
            keep1[t, :, pl.ds(lo, half1)] = value[0]

        x_in("b1x", t, xr1, part1(t), half1, finish)
        net.send(f"b1z{t}", zs1.at[t], zr1.at[t], zn)

    def sum2_1(t):
        net.arrived(f"b2c{t}")
        for k in range(4):
            zs2[t, k] = (own2[t, 2 * k + 1] + got2[t, 2 * k + 1].astype(F32)).astype(BF16)
        net.send(f"b2z{t}", zs2.at[t], zr2.at[t], zn)

    def sum2_2(t):
        net.arrived(f"b2z{t}")
        x_out("b2x", t, xs2, xr2, part2(t), half2)

    def sum2_3(t):
        x_on("b2x", t, xs2, xr2, part2(t), half2)

    def swiglu_back(t, hidden, grads, lo, offset):
        width = hidden.shape[-1]
        here = (pl.ds(t * rows, rows), pl.ds(offset + lo, width))
        gate, up = gv[here].astype(F32), uv[here].astype(F32)
        s = jax.nn.sigmoid(gate)
        there = pl.ds(lo, width)
        grads[t, 1, 0, 0, :, there] = (hidden * gate * s).astype(BF16)
        grads[t, 0, 0, 0, :, there] = (
            hidden * up * s * (1.0 + gate * (1.0 - s))
        ).astype(BF16)

    def sum1_4(t):
        net.arrived(f"b1z{t}")
        for lo in range(0, wide1, LANES):
            there = pl.ds(lo, LANES)
            hidden = keep1[t, :, there] + zr1[t, :, there].astype(F32)
            swiglu_back(t, hidden, grads1, lo, 0)

    def sum2_4(t):
        def finish(lo, value):
            swiglu_back(t, value, grads2, lo, wide1)

        x_in("b2x", t, xr2, part2(t), half2, finish)

    def block(grads, t, core_, e, lo=None, width=None):
        if lo is None:
            return grads.at[t, :, core_, e]
        return grads.at[t, :, core_, e, :, pl.ds(lo, width)]

    def to_core(name, grads, t, e):
        net.send(f"{name}p{e}{t}", block(grads, t, 0, e), block(grads, t, 1, e), core)

    def to_x(name, grads, t, z_):
        net.send(f"{name}x{6 + z_}{t}", block(grads, t, 0, z_), block(grads, t, 0, 6 + z_), xp)
        net.send(f"{name}x{2 + z_}{t}", block(grads, t, 0, z_), block(grads, t, 0, 2 + z_), xm)

    def on_x(name, grads, t, z_, half):
        net.arrived(f"{name}x{6 + z_}{t}")
        net.send(
            f"{name}l{z_}{t}",
            block(grads, t, 0, 6 + z_, 0, half),
            block(grads, t, 0, 4 + z_, 0, half),
            xp,
        )
        net.arrived(f"{name}x{2 + z_}{t}")
        net.send(
            f"{name}r{z_}{t}",
            block(grads, t, 0, 2 + z_, half, half),
            block(grads, t, 0, 4 + z_, half, half),
            xm,
        )

    def to_z(name, grads, t, e):
        net.send(f"{name}z{e}{t}", block(grads, t, 0, e), block(grads, t, 0, e + 1), zn)

    def all1_1(t):
        to_z("c1", grads1, t, 0)
        to_x("c1", grads1, t, 0)
        to_core("c1", grads1, t, 0)

    def all1_2(t):
        net.arrived(f"c1z0{t}")
        to_x("c1", grads1, t, 1)
        to_core("c1", grads1, t, 1)

    def all1_3(t):
        for z_ in range(2):
            on_x("c1", grads1, t, z_, half1)
            to_core("c1", grads1, t, 6 + z_)
            to_core("c1", grads1, t, 2 + z_)

    def all1_4(t):
        for z_ in range(2):
            net.arrived(f"c1l{z_}{t}", f"c1r{z_}{t}")
            to_core("c1", grads1, t, 4 + z_)

    def all1_5(t):
        net.arrived(*(f"c1p{e}{t}" for e in range(8)))

    def all2_1(t):
        to_x("c2", grads2, t, 0)
        to_z("c2", grads2, t, 0)
        to_core("c2", grads2, t, 0)

    def all2_2(t):
        on_x("c2", grads2, t, 0, half2)
        for e in (6, 2):
            to_z("c2", grads2, t, e)
            to_core("c2", grads2, t, e)

    def all2_3(t):
        net.arrived(f"c2l0{t}", f"c2r0{t}")
        to_z("c2", grads2, t, 4)
        to_core("c2", grads2, t, 4)

    def all2_4(t):
        for e in (0, 6, 2, 4):
            net.arrived(f"c2z{e}{t}")
            to_core("c2", grads2, t, e + 1)

    def all2_5(t):
        net.arrived(*(f"c2p{e}{t}" for e in range(8)))

    def second_dot(t, grads, offset, first):
        def tile(n, carry):
            there = pl.ds(pl.multiple_of(n * LANES, LANES), LANES)
            here = (there, pl.ds(offset, grads.shape[-1]))
            wide = grads.shape[-1]
            share = contract_last(grads[t, 0].reshape(16 * rows, wide), wg[here])
            share += contract_last(grads[t, 1].reshape(16 * rows, wide), wu[here])
            share = share.reshape(2, 8, rows, LANES)
            total[t, :, :, :, there] = share if first else total[t, :, :, :, there] + share
            return carry

        lax.fori_loop(0, total.shape[-1] // LANES, tile, 0)

    def dot_3(t):
        second_dot(t, grads1, 0, True)

    def dot_4(t):
        second_dot(t, grads2, wide1, False)

    def part3(t, j, lo):
        return [
            total[t, :, place((zh + za) % 2, y + j), :, pl.ds(lo, half3)] for za in range(2)
        ]

    def down_1(t):
        for way, m, j, lo, to in (
            (0, 0, 2, 0, yp), (1, 0, 2, half3, ym), (0, 1, 1, half3, yp), (1, 1, 3, 0, ym),
        ):
            for za, value in enumerate(part3(t, j, lo)):
                ys[t, way, m, za] = value.astype(BF16)
            net.send(f"d{way}{m}{t}", ys.at[t, way, m], yr.at[t, way, m], to)

    def down_2(t):
        for way, j, lo, to in ((0, 1, 0, yp), (1, 3, half3, ym)):
            net.arrived(f"d{way}0{t}")
            for za, value in enumerate(part3(t, j, lo)):
                ys[t, way, 2, za] = (value + yr[t, way, 0, za].astype(F32)).astype(BF16)
            net.send(f"d{way}2{t}", ys.at[t, way, 2], yr.at[t, way, 2], to)

    def down_3(t):
        net.arrived(*(f"d{way}{m}{t}" for way in (0, 1) for m in (1, 2)))
        for lo, m in ((0, 2), (half3, 1)):
            for za, value in enumerate(part3(t, 0, lo)):
                value = (
                    value
                    + yr[t, 0, m, za].astype(F32)
                    + yr[t, 1, 3 - m, za].astype(F32)
                )
                if za:
                    hs[t, :, :, pl.ds(lo, half3)] = value.astype(BF16)
                else:
                    keep3[t, :, :, pl.ds(lo, half3)] = value
        net.send(f"dz{t}", hs.at[t], hr.at[t], zp)

    def down_4(t):
        net.arrived(f"dz{t}")
        value = (keep3[t] + hr[t].astype(F32)).astype(BF16)
        for c_ in range(2):
            out[(c_ + c) % 2, pl.ds(t * rows, rows), :] = value[c_]

    for t in range(CHUNKS):
        gather_1(t)
    for t in range(CHUNKS):
        gather_2(t)
        gather_3(t)
    gather_4(0)
    gather_5(0)
    loads["d2"].wait()
    dot_2(0)
    gather_4(1)
    loads["d1"].wait()
    dot_1(0)
    gather_5(1)
    sum2_1(0)
    dot_2(1)
    sum1_1(0)
    sum2_2(0)
    dot_1(1)
    sum1_2(0)
    sum2_3(0)
    sum2_1(1)
    sum1_1(1)
    sum1_3(0)
    loads["gv"].wait()
    loads["uv"].wait()
    sum2_4(0)
    all2_1(0)
    sum2_2(1)
    sum1_2(1)
    sum1_4(0)
    all1_1(0)
    sum2_3(1)
    sum1_3(1)
    all2_2(0)
    all1_2(0)
    sum2_4(1)
    all2_1(1)
    sum1_4(1)
    all1_1(1)
    all2_3(0)
    all1_3(0)
    all2_2(1)
    all1_2(1)
    all1_4(0)
    all2_4(0)
    all2_3(1)
    all1_3(1)
    all1_5(0)
    loads["wg"].wait()
    loads["wu"].wait()
    dot_3(0)
    all1_4(1)
    all2_5(0)
    dot_4(0)
    all2_4(1)
    down_1(0)
    all1_5(1)
    dot_3(1)
    down_2(0)
    all2_5(1)
    down_3(0)
    dot_4(1)
    down_1(1)
    down_4(0)
    down_2(1)
    down_3(1)
    down_4(1)
    net.finish()


def solution(mesh):
    assert mesh.shape["row"] == 16 and mesh.shape["col"] == 8

    def per_device(out_grad, gate_saved, up_saved, gate_weight, up_weight, down_weight):
        hidden = gate_saved.shape[1]
        depth = out_grad.shape[1]
        tiles = hidden // LANES
        wide1 = (tiles + 1) // 2 * LANES
        wide2 = hidden - wide1
        rows = gate_saved.shape[0] // CHUNKS
        n = CHUNKS
        scratch = [
            pltpu.VMEM((n, 2, 8, rows, depth), BF16),
            pltpu.VMEM(down_weight.shape, BF16),
            pltpu.VMEM(gate_weight.shape, BF16),
            pltpu.VMEM(up_weight.shape, BF16),
            pltpu.VMEM(gate_saved.shape, BF16),
            pltpu.VMEM(up_saved.shape, BF16),
            pltpu.VMEM((n, 8, rows, wide1), F32),
            pltpu.VMEM((n, 8, rows, wide2), F32),
            pltpu.VMEM((n, 8, rows, wide1), BF16),
            pltpu.VMEM((n, 8, rows, wide2), BF16),
            pltpu.VMEM((n, 8, rows, wide1), BF16),
            pltpu.VMEM((n, 8, rows, wide2), BF16),
            pltpu.VMEM((n, 2, 3, 2, rows, wide1 // 2), BF16),
            pltpu.VMEM((n, 2, 3, 2, rows, wide1 // 2), BF16),
            pltpu.VMEM((n, 2, 3, rows, wide2 // 2), BF16),
            pltpu.VMEM((n, 2, 3, rows, wide2 // 2), BF16),
            pltpu.VMEM((n, rows, wide1), BF16),
            pltpu.VMEM((n, rows, wide1), BF16),
            pltpu.VMEM((n, rows, wide1), F32),
            pltpu.VMEM((n, 4, rows, wide2), BF16),
            pltpu.VMEM((n, 4, rows, wide2), BF16),
            pltpu.VMEM((n, 2, 2, 8, rows, wide1), BF16),
            pltpu.VMEM((n, 2, 2, 8, rows, wide2), BF16),
            pltpu.VMEM((n, 2, 8, rows, depth), F32),
            pltpu.VMEM((n, 2, 3, 2, 2, rows, depth // 2), BF16),
            pltpu.VMEM((n, 2, 3, 2, 2, rows, depth // 2), BF16),
            pltpu.VMEM((n, 2, rows, depth), F32),
            pltpu.VMEM((n, 2, rows, depth), BF16),
            pltpu.VMEM((n, 2, rows, depth), BF16),
            pltpu.SemaphoreType.DMA((6 + 2 * n,)),
            pltpu.SemaphoreType.DMA((70 * n,)),
            pltpu.SemaphoreType.DMA((70 * n,)),
        ]
        result = pl.pallas_call(
            kernel,
            out_shape=jax.ShapeDtypeStruct((2, gate_saved.shape[0], depth), BF16),
            in_specs=[pl.BlockSpec(memory_space=pl.ANY)] * 6,
            out_specs=pl.BlockSpec(memory_space=pltpu.VMEM),
            scratch_shapes=scratch,
            compiler_params=pltpu.CompilerParams(
                collective_id=0,
                has_side_effects=True,
                vmem_limit_bytes=60 * 1024 * 1024,
            ),
        )(out_grad, gate_saved, up_saved, gate_weight, up_weight, down_weight)
        return result.reshape(out_grad.shape)

    placed = (
        P("col", "row"),
        P("row", "col"),
        P("row", "col"),
        P("row", "col"),
        P("row", "col"),
        P("col", "row"),
    )
    return jax.shard_map(
        per_device, mesh=mesh, in_specs=placed, out_specs=P("col", "row"), check_vma=False
    )
```
